32 devices in a mesh: groups: 2 (over x), tm: 16 (over z, y, core).
Axes of the slice: x: 2, y: 2, z: 4, core: 2. Of those that a mesh axis runs over, the one named last changes fastest.
Arguments:
- coupling: bfloat16 [1024, 1024], replicated, may hold values from -0.0546875 to 0.0546875
- decay: float32 [32, 1024], P(('groups', 'tm')), parts along dimension 0, may hold values from 0.3 to 1
- block_mask: int32 [32, 8, 8], P(('groups', 'tm')), parts along dimension 0, may hold values 0 or 1
- gain: bfloat16 [1024, 256], replicated, may hold values from -0.375 to 0.375
- readings: bfloat16 [32, 256, 2048], P(('groups', 'tm')), parts along dimension 0, may hold values from -6 to 6
- influence: float32 [1024, 4], replicated, may hold values from -6 to 6
- lanes: int32 [32, 2048], P(('groups', 'tm')), parts along dimension 0, may hold values from 0 to 3
- axle_load: float32 [32, 2048], P(('groups', 'tm')), parts along dimension 0, may hold values from -6 to 6
Outputs:
- states: float32 [32, 1024, 2048], P(('groups', 'tm')), parts along dimension 0
The draws below stay inside these ranges and needn't reach their ends.
There are 2 independent parts, one for each index of `groups`. The reference program is written for one: setup_inputs(seed, part) draws one part's arguments, and reference() takes and returns one part's arrays. A program takes and returns all parts, laid end to end along the dimension named above; an argument that names none is the same for every part. Nothing has to cross between parts.
Inputs may be any that keep to these rules, and one draw needn't show every extreme that they name: `block_mask`: 1 where the time block couples a block of states to another.
All inputs are finite; a program needn't handle non-finite values.
Results may differ from the reference program's by a relative error of at most 0.006.
Values may be sent and summed in bfloat16 or wider, within the bound.
No kernel may reach another device: no remote copies, remote signals or barrier semaphores. Data moves between devices by JAX's collectives and lax.ppermute only.
A program may use at most 64 MiB of HBM per device.

```python
import math
import jax
import jax.numpy as jnp
from jax import lax

N = 1024
SENS = 256
LANES = 4
SCEN = 2048
NBK = 8
NT = 16


def touch_ends(drawn, own_key, low, largest):
    longest = drawn.shape.index(max(drawn.shape))
    spots = []
    for shift in (0, 1):
        where = [jax.random.randint(jax.random.fold_in(own_key, axis), (), 0, length) for axis, length in enumerate(drawn.shape)]
        where[longest] = (where[longest] + shift) % drawn.shape[longest]
        spots.append(tuple(where))
    return drawn.at[spots[0]].set(low).at[spots[1]].set(largest)


def level_of(key, dims, split, least, high):
    def one(dim, parts):
        draws = jax.random.uniform(jax.random.fold_in(jax.random.fold_in(key, 6), dim), (parts,), jnp.float32, least / len(split), high / len(split))
        return jnp.repeat(jnp.exp(draws), dims[dim] // parts).reshape((-1,) + (1,) * (len(dims) - dim - 1))

    level = one(*split[0])
    for cut in split[1:]:
        level = level * one(*cut)
    return level


def scatter_about(stream_key, extent, deviation, limit, pieces=(), kind=jnp.bfloat16):
    values = jax.random.normal(stream_key, extent, jnp.float32) * deviation
    if len(pieces) > 0:
        values = level_of(stream_key, extent, pieces, -0.22, 0.18) * values
    return jnp.clip(values, min=-limit, max=limit).astype(kind)


def setup_inputs(seed: int = 0, part: int = 0) -> dict:
    streams_of = jax.random.split(jax.random.key(seed), 9)
    own_keys = jax.random.split(jax.random.fold_in(streams_of[8], part), 9)
    coupling = scatter_about(streams_of[0], (N, N), (12 * N) ** -0.5, 0.0546875)
    decay = jnp.clip(jnp.exp(math.log(1.0) - 1.2039728 * jax.random.uniform(own_keys[1], (NT, N), jnp.float32) ** level_of(own_keys[1], (NT, N), ((0, 16),), -0.2, 0.2)), 0.3, 1.0)
    block_mask = touch_ends((jax.random.randint(own_keys[2], (NT, NBK, NBK), 0, 2) < 1).astype(jnp.int32), jax.random.fold_in(own_keys[2], 1), 0, 1)
    gain = scatter_about(streams_of[3], (N, SENS), SENS ** -0.5, 0.375)
    readings = scatter_about(own_keys[4], (NT, SENS, SCEN), 1.0, 6.0, ((0, 16),))
    influence = scatter_about(streams_of[5], (N, LANES), 1.0, 6.0, (), jnp.float32)
    lanes = touch_ends(jax.random.randint(own_keys[6], (NT, SCEN), 0, LANES), jax.random.fold_in(own_keys[6], 1), 0, LANES - 1).astype(jnp.int32)
    axle_load = scatter_about(own_keys[7], (NT, SCEN), 1.0, 6.0, ((0, 16),), jnp.float32)
    return dict(coupling=coupling, decay=decay, block_mask=block_mask, gain=gain, readings=readings, influence=influence, lanes=lanes, axle_load=axle_load)


def build(coupling, rate_row, mask_row):
    blocks = mask_row.shape[0]
    width = coupling.shape[0]
    size = width // blocks
    masked = coupling.astype(jnp.float32).reshape(blocks, size, blocks, size) * mask_row.astype(jnp.float32)[:, None, :, None]
    return (masked.reshape(width, width) + jnp.diag(rate_row.astype(jnp.float32))).astype(jnp.bfloat16)


def shift_back(values, dist):
    front = jnp.zeros((dist,) + values.shape[1:], values.dtype)
    return jnp.concatenate([front, values[:-dist]], axis=0)


def multiply(left, right):
    return jnp.einsum("tij,tjk->tik", left.astype(jnp.float32), right.astype(jnp.float32), precision=lax.Precision.HIGHEST)


def reference(coupling, decay, block_mask, gain, readings, influence, lanes, axle_load):
    rate = decay.astype(jnp.bfloat16)
    trans = jax.vmap(lambda row, mrow: build(coupling, row, mrow))(rate, block_mask)
    sensed = jnp.einsum("ns,tsr->tnr", gain.astype(jnp.float32), readings.astype(jnp.float32), precision=lax.Precision.HIGHEST)
    picks = (lanes[:, None, :] == jnp.arange(LANES, dtype=jnp.int32)[None, :, None]).astype(jnp.float32) * axle_load[:, None, :]
    drive = sensed + jnp.einsum("nl,tlr->tnr", influence, picks, precision=lax.Precision.HIGHEST)
    pair = multiply(trans, shift_back(trans, 1)).astype(jnp.bfloat16)
    sum_one = drive + multiply(trans, shift_back(drive.astype(jnp.bfloat16), 1))
    quad = multiply(pair, shift_back(pair, 2)).astype(jnp.bfloat16)
    sum_two = sum_one + multiply(pair, shift_back(sum_one.astype(jnp.bfloat16), 2))
    return sum_two + multiply(quad, shift_back(sum_two.astype(jnp.bfloat16), 4))
```

```python
import functools

import jax
import jax.numpy as jnp
from jax import lax
from jax.experimental import pallas as pl
from jax.experimental.pallas import tpu as pltpu
from jax.sharding import PartitionSpec as P

MIB = 1 << 20
VMEM = pl.BlockSpec(memory_space=pltpu.VMEM)
ANY = pl.BlockSpec(memory_space=pl.ANY)
F32 = jnp.float32
BF16 = jnp.bfloat16
LAGS = 8
ROWS = 16


def position():
    return lax.rem(lax.axis_index("tm"), 4)


def send(block, pairs, levels):
    count = lax.axis_size("tm")
    route = []
    for level in range(count // 4):
        for a, b, step in pairs:
            if level + step < count // 4:
                route.append((level * 4 + a, (level + step) * 4 + b))
    return lax.ppermute(block, "tm", route)


CORE = [(0, 1, 0), (1, 0, 0), (2, 3, 0), (3, 2, 0)]
ROW = [(0, 2, 0), (2, 0, 0), (1, 3, 0), (3, 1, 0)]
ROW0 = [(0, 2, 0), (2, 0, 0)]
ROW1 = [(1, 3, 0), (3, 1, 0)]


def record_of(j, lag, recs):
    d = j - lag
    pos = lax.rem(d + 8, 4)
    here = recs[0][pos ^ j]
    base = j | 1
    row = jnp.where(d >= 0, here, recs[1][pos ^ base])
    if len(recs) > 2:
        row = jnp.where(d >= -4, row, recs[2][pos ^ base])
    return row.astype(F32)


def build(c_ref, rec, t_ref):
    width = c_ref.shape[0]
    size = width // 8
    eye = (
        lax.broadcasted_iota(jnp.int32, (size, size), 0)
        == lax.broadcasted_iota(jnp.int32, (size, size), 1)
    ).astype(F32)
    for p in range(8):
        rows = slice(p * size, (p + 1) * size)
        masked = c_ref[rows, :].astype(F32) * rec[p : p + 1, :]
        t_ref[rows, :] = masked.astype(BF16)
        rate = rec[8:9, p * size : (p + 1) * size]
        t_ref[rows, rows] = (masked[:, rows] + eye * rate).astype(BF16)


def times(left, right):
    return jnp.dot(left, right, preferred_element_type=F32)


def keep(m_ref, w, value, lag, sens):
    m_ref[:, lag * sens : (lag + 1) * sens] = value[:, :sens].astype(BF16)
    lanes = lax.broadcasted_iota(jnp.int32, w.shape, 1)
    mine = ((lanes & 31) >> 2) == lag
    return jnp.where(mine, value[:, sens:], w)


def extend(p_ref, t_ref, out_ref):
    width = p_ref.shape[0]
    for n in range(0, width, 256):
        out_ref[:, n : n + 256] = times(p_ref[...], t_ref[:, n : n + 256]).astype(BF16)


def first_kernel(c, gi, inf, s0, s1, m, w, p2, t1, t2):
    sens = gi.shape[1] - 128
    j = position()
    m[:, :sens] = gi[:, :sens]
    build(c, record_of(j, 0, (s0, s1)), t1)
    acc = keep(m, inf[...], times(t1[...], gi[...]), 1, sens)
    build(c, record_of(j, 1, (s0, s1)), t2)
    extend(t1, t2, p2)
    w[...] = keep(m, acc, times(p2[...], gi[...]), 2, sens)


def next_kernel(lag, c, gi, s0, s1, p, m_in, w_in, m, w, q, t):
    del m_in
    sens = gi.shape[1] - 128
    build(c, record_of(position(), lag, (s0, s1)), t)
    extend(p, t, q)
    w[...] = keep(m, w_in[...], times(q[...], gi[...]), lag + 1, sens)


def far_kernel(c, gi, s0, s1, s2, f5, f6, f7, fw, t):
    sens = gi.shape[1] - 128
    j = position()
    recs = (s0, s1, s2)
    f7[...] = gi[:, :sens]
    f6[...] = gi[:, :sens]
    f5[...] = gi[:, :sens]
    fw[...] = gi[:, sens:]
    lanes = lax.broadcasted_iota(jnp.int32, fw.shape, 1)
    group = (lanes & 31) >> 2
    for lag in (6, 5, 4):
        build(c, record_of(j, lag, recs), t)
        f7[...] = times(t[...], f7[...]).astype(BF16)
        if lag < 6:
            f6[...] = times(t[...], f6[...]).astype(BF16)
        if lag < 5:
            f5[...] = times(t[...], f5[...]).astype(BF16)
        fw[...] = jnp.where(group > lag, times(t[...], fw[...]).astype(BF16), fw[...])


def near_kernel(p, f5, f6, f7, fw, m_in, w_in, m, w):
    del m_in
    sens = f5.shape[1]
    for lag, f in ((5, f5), (6, f6), (7, f7)):
        m[:, lag * sens : (lag + 1) * sens] = times(p[...], f[...]).astype(BF16)
    lanes = lax.broadcasted_iota(jnp.int32, w_in.shape, 1)
    full = jnp.where(((lanes & 31) >> 2) >= 5, times(p[...], fw[...]), w_in[...])
    high = full.astype(BF16)
    low = (full - high.astype(F32)).astype(BF16)
    w[...] = jnp.where(lanes < 64, high, jnp.where(lanes < 96, low, jnp.zeros_like(low)))


def picks_kernel(s0, s1, s2, out, tmp):
    j = position()
    half = s0.shape[2]
    tmp[96:, :] = jnp.zeros_like(tmp[96:, :])
    for lag in range(LAGS):
        rec = record_of(j, lag, (s0, s1, s2))
        for h in range(2):
            cols = slice(h * half, (h + 1) * half)
            lane = lax.broadcasted_iota(jnp.int32, (4, half), 0).astype(F32)
            mine = lane == rec[9 + h : 10 + h, :]
            high = jnp.where(mine, rec[11 + h : 12 + h, :], 0.0)
            low = jnp.where(mine, rec[13 + h : 14 + h, :], 0.0)
            tmp[4 * lag : 4 * lag + 4, cols] = high
            tmp[32 + 4 * lag : 36 + 4 * lag, cols] = low
            tmp[64 + 4 * lag : 68 + 4 * lag, cols] = high
    out[...] = tmp[...].astype(BF16)


EARLY = {
    0: [(0, "O"), (1, "CYR2"), (2, "YR1"), (3, "CR2"), (4, "R1")],
    1: [(0, "O"), (1, "CO"), (2, "YR2"), (3, "CYR1"), (4, "R2"), (5, "CR1")],
    2: [(0, "O"), (2, "YO1"), (3, "CR2"), (4, "R1"), (5, "CYR2"), (6, "YR1")],
    3: [(0, "O"), (1, "CO"), (3, "CYO1"), (4, "R2"), (5, "CR1"), (6, "YR2"), (7, "CYR1")],
}
LATE = {
    0: [(5, "Y6"), (6, "CZ3"), (7, "Z2")],
    1: [(6, "CY6"), (7, "Z3")],
    2: [(1, "CYO2"), (7, "Z2")],
    3: [(2, "YO2")],
}


def names_of(table):
    return sorted({name for entries in table.values() for _, name in entries})


def runs_of(entries):
    runs = []
    for lag, _ in entries:
        if runs and runs[-1][1] == lag:
            runs[-1][1] = lag + 1
        else:
            runs.append([lag, lag + 1])
    return runs


def sum_kernel(table, has_loads, cols, steps, *refs):
    names = names_of(table)
    blocks = dict(zip(names, refs[: len(names)]))
    rest = list(refs[len(names) :])
    m = rest.pop(0)
    if has_loads:
        w, picks = rest.pop(0), rest.pop(0)
    else:
        start = rest.pop(0)
    out, held, sems = rest
    sens = held.shape[1] // LAGS
    j = position()
    i = pl.program_id(0)
    now = lax.rem(i, 2)

    def copies(step, slot, entries):
        where = pl.ds(pl.multiple_of(step * cols, cols), cols)
        return [
            pltpu.make_async_copy(
                blocks[name].at[:sens, where],
                held.at[slot, pl.ds(lag * sens, sens), :],
                sems.at[slot, lag],
            )
            for lag, name in entries
        ]

    for pos, entries in table.items():

        @pl.when(j == pos)
        def _(entries=entries):
            @pl.when(i == 0)
            def _():
                for copy in copies(0, 0, entries):
                    copy.start()

            @pl.when(i + 1 < steps)
            def _():
                for copy in copies(i + 1, 1 - now, entries):
                    copy.start()

            for copy in copies(i, now, entries):
                copy.wait()
            total = times(w[...], picks[...]) if has_loads else start[...]
            for lo, hi in runs_of(entries):
                total += times(
                    m[:, lo * sens : hi * sens], held[now, lo * sens : hi * sens, :]
                )
            out[...] = total


def call(kernel, outs, ins, scratch=(), aliases=None, flops=0, limit=24):
    moved = sum(a.size * a.dtype.itemsize for a in ins)
    return pl.pallas_call(
        kernel,
        out_shape=outs,
        in_specs=[VMEM] * len(ins),
        out_specs=[VMEM] * len(outs),
        scratch_shapes=list(scratch),
        input_output_aliases=aliases or {},
        cost_estimate=pl.CostEstimate(flops=flops, bytes_accessed=moved, transcendentals=0),
        compiler_params=pltpu.CompilerParams(vmem_limit_bytes=limit * MIB),
    )(*ins)


def call_sum(table, blocks, m, extra, width, scen):
    names = names_of(table)
    sens = m.shape[1] // LAGS
    cols = 512
    steps = scen // cols
    has_loads = len(extra) == 2
    full = lambda a: pl.BlockSpec(a.shape, lambda i: (0, 0), pipeline_mode=pl.Buffered(1))
    across = lambda a: pl.BlockSpec((a.shape[0], cols), lambda i: (0, i))
    specs = [ANY] * len(names) + [full(m)]
    specs += [full(extra[0]), across(extra[1])] if has_loads else [across(extra[0])]
    return pl.pallas_call(
        functools.partial(sum_kernel, table, has_loads, cols, steps),
        grid=(steps,),
        out_shape=jax.ShapeDtypeStruct((width, scen), F32),
        in_specs=specs,
        out_specs=pl.BlockSpec((width, cols), lambda i: (0, i)),
        scratch_shapes=[
            pltpu.VMEM((2, LAGS * sens, cols), BF16),
            pltpu.SemaphoreType.DMA((2, LAGS)),
        ],
        cost_estimate=pl.CostEstimate(
            flops=2 * width * scen * sens * max(len(e) for e in table.values()),
            bytes_accessed=16 * MIB,
            transcendentals=0,
        ),
        compiler_params=pltpu.CompilerParams(vmem_limit_bytes=30 * MIB),
    )(*[blocks[n] for n in names], m, *extra)


def per_device(coupling, decay, block_mask, gain, readings, influence, lanes, axle_load):
    width, sens = gain.shape
    scen = readings.shape[2]
    lane_count = influence.shape[1]
    core = lax.rem(lax.axis_index("tm"), 2)
    own = readings[0]
    shape = jax.ShapeDtypeStruct

    high = axle_load.astype(BF16)
    low = (axle_load - high.astype(F32)).astype(BF16)
    half = scen // 2
    record = jnp.concatenate(
        [
            jnp.repeat(block_mask[0].astype(BF16), width // 8, axis=1),
            decay.astype(BF16),
            lanes.astype(BF16).reshape(2, half),
            high.reshape(2, half),
            low.reshape(2, half),
            jnp.zeros((1, half), BF16),
        ],
        axis=0,
    )[None]
    spread = jnp.tile(influence, (1, 128 // lane_count))
    gi = jnp.concatenate([gain, spread.astype(BF16)], axis=1)

    r = {"O": own}
    r["R1"] = send(own, [(0, 0, 1), (2, 2, 1)], None)
    r["CO"] = send(own, CORE, None)
    pair = jnp.concatenate([record, send(record, CORE, None)], axis=0)
    s0 = jnp.concatenate([pair, send(pair, ROW, None)], axis=0)
    s1 = send(s0, [(1, 1, 1), (3, 3, 1)], None)
    s1 = jnp.where(core == 1, s1, send(s1, CORE, None))
    r["YO1"] = send(own, ROW0, None)

    small = shape((width, 128), F32)
    p_shape = shape((width, width), BF16)
    m_shape = shape((width, LAGS * sens), BF16)
    unit = 2 * width * width * 256
    t_scratch = pltpu.VMEM((width, width), BF16)

    load = jnp.concatenate([own, s1.reshape(-1, scen)], axis=0)
    r2 = send(load, [(1, 1, 1), (3, 3, 1)], None)
    m, w, p = call(
        first_kernel, [m_shape, small, p_shape], [coupling, gi, spread, s0, s1],
        [t_scratch, t_scratch], flops=8 * unit,
    )
    r["CYO1"] = send(r["YO1"], CORE, None)
    r["CR1"] = send(r["R1"], CORE, None)
    r["YR1"] = send(r["R1"], ROW0, None)
    r["CYR1"] = send(r["YR1"], CORE, None)
    r["Z3"] = send(r["YR1"], [(0, 1, 1)], None)
    r["CZ3"] = send(r["Z3"], CORE, None)
    r["R2"] = r2[:sens]
    s2 = r2[sens:].reshape(s1.shape)
    s2 = jnp.where(core == 1, s2, send(s2, CORE, None))
    r["CR2"] = send(r["R2"], CORE, None)
    r["YR2"] = send(r["R2"], ROW1, None)
    r["CYR2"] = send(r["YR2"], CORE, None)
    r["Z2"] = send(r["R2"], [(1, 0, 1), (3, 2, 1)], None)
    r["Y6"] = send(r["Z2"], [(2, 0, 0)], None)
    r["CY6"] = send(r["Y6"], CORE, None)
    r["YO2"] = send(own, [(1, 3, 0)], None)
    r["CYO2"] = send(r["YO2"], CORE, None)

    for lag in (2, 3):
        m, w, p = call(
            functools.partial(next_kernel, lag), [m_shape, small, p_shape],
            [coupling, gi, s0, s1, p, m, w], [t_scratch], {5: 0, 6: 1}, flops=6 * unit,
        )
    f_shape = shape((width, sens), BF16)
    f5, f6, f7, fw = call(
        far_kernel, [f_shape, f_shape, f_shape, shape((width, 128), BF16)],
        [coupling, gi, s0, s1, s2], [t_scratch], flops=9 * unit,
    )
    m, w = call(
        near_kernel, [m_shape, shape((width, 128), BF16)],
        [p, f5, f6, f7, fw, m, w], (), {5: 0}, flops=4 * unit,
    )
    (picks,) = call(
        picks_kernel, [shape((128, scen), BF16)], [s0, s1, s2],
        [pltpu.VMEM((128, scen), F32)], flops=MIB,
    )
    early = call_sum(EARLY, r, m, (w, picks), width, scen)
    states = call_sum(LATE, r, m, (early,), width, scen)
    return states[None]


def solution(mesh):
    placed = (
        P(),
        P(("groups", "tm"), None),
        P(("groups", "tm"), None, None),
        P(),
        P(("groups", "tm"), None, None),
        P(),
        P(("groups", "tm"), None),
        P(("groups", "tm"), None),
    )
    return jax.shard_map(
        per_device,
        mesh=mesh,
        in_specs=placed,
        out_specs=P(("groups", "tm"), None, None),
        check_vma=False,
    )
```

```python
import functools

import jax
import jax.numpy as jnp
from jax import lax
from jax.experimental import pallas as pl
from jax.experimental.pallas import tpu as pltpu
from jax.sharding import PartitionSpec as P

MIB = 1 << 20
LIMIT = 20 * MIB
VMEM = pl.BlockSpec(memory_space=pltpu.VMEM)
ANY = pl.BlockSpec(memory_space=pl.ANY)
F32 = jnp.float32
BF16 = jnp.bfloat16
LAGS = 8
COLS = 256
ROWS = 8


def position():
    return lax.rem(lax.axis_index("tm"), 4)


def send(block, pairs):
    count = lax.axis_size("tm")
    route = []
    for level in range(count // 4):
        for a, b, step in pairs:
            if level + step < count // 4:
                route.append((level * 4 + a, (level + step) * 4 + b))
    return lax.ppermute(block, "tm", route)


def after(block, *others):
    return lax.optimization_barrier((block, *others))[0]


CORE = [(0, 1, 0), (1, 0, 0), (2, 3, 0), (3, 2, 0)]
ROW = [(0, 2, 0), (2, 0, 0), (1, 3, 0), (3, 1, 0)]
ROW0 = [(0, 2, 0), (2, 0, 0)]
ALL = [(0, 0, 1), (1, 1, 1), (2, 2, 1), (3, 3, 1)]
ROW1 = [(1, 3, 0), (3, 1, 0)]


def record_of(j, lag, near, far=None, swapped=None):
    d = j - lag
    pos = lax.rem(d + 8, 4)
    row = jnp.where(d >= 0, near[0, pos ^ (j | 1)], near[1, pos ^ (j | 1)])
    if far is not None:
        held = jnp.where((j & 1) == 0, far[pos ^ (j | 1)], swapped[pos ^ (j | 1)])
        row = jnp.where(d >= -4, row, held)
    return row.astype(F32)


def call(kernel, outs, ins, scratch=(), flops=0, spec=VMEM, limit=LIMIT):
    moved = sum(a.size * a.dtype.itemsize for a in ins)
    return pl.pallas_call(
        kernel,
        out_shape=outs,
        in_specs=[spec] * len(ins),
        out_specs=[VMEM] * len(outs),
        scratch_shapes=list(scratch),
        cost_estimate=pl.CostEstimate(flops=flops, bytes_accessed=moved, transcendentals=0),
        compiler_params=pltpu.CompilerParams(vmem_limit_bytes=limit),
    )(*ins)


def build(c_ref, rec, t_ref):
    width = t_ref.shape[0]
    size = width // 8
    eye = (
        lax.broadcasted_iota(jnp.int32, (size, size), 0)
        == lax.broadcasted_iota(jnp.int32, (size, size), 1)
    ).astype(F32)
    for p in range(8):
        rows = slice(p * size, (p + 1) * size)
        half = p % 2 * width
        masked = c_ref[rows, :].astype(F32) * rec[p // 2 : p // 2 + 1, half : half + width]
        t_ref[rows, :] = masked.astype(BF16)
        rate = rec[4:5, p * size : (p + 1) * size]
        t_ref[rows, rows] = (masked[:, rows] + eye * rate).astype(BF16)


def times(left, right):
    return jnp.dot(left, right, preferred_element_type=F32)


def split(value, m, w):
    sens = m.shape[1]
    m[...] = value[:, :sens].astype(BF16)
    w[...] = value[:, sens:]


def record_kernel(decay, mask, lanes, load, out, *scratch):
    held, sems = scratch[:4], scratch[4]
    moves = [
        pltpu.make_async_copy(source, target, sems.at[i])
        for i, (source, target) in enumerate(zip((decay, mask, lanes, load), held))
    ]
    for move in moves:
        move.start()
    for move in moves:
        move.wait()
    decay, mask, lanes, load = held
    width = decay.shape[1]
    size = width // 8
    flags = mask[...]
    for q in range(8):
        wide = jnp.broadcast_to(flags[0, :, q : q + 1].astype(F32), (8, size)).astype(BF16)
        for p in range(8):
            first = p % 2 * width + q * size
            out[0, p // 2 : p // 2 + 1, first : first + size] = wide[p : p + 1]
    rate = decay[...]
    loads = load[...]
    high = loads.astype(BF16).astype(F32)
    rows = [jnp.concatenate([rate, jnp.zeros_like(rate)], axis=1)]
    rows += [lanes[...].astype(F32), high, loads - high]
    out[0, 4:, :] = jnp.concatenate(rows, axis=0).astype(BF16)


def load_kernel(c, gain, inf, c_out, gi, spread, inf_held, sems):
    sens = gain.shape[1]
    moves = [
        pltpu.make_async_copy(c, c_out, sems.at[0]),
        pltpu.make_async_copy(gain, gi.at[:, :sens], sems.at[1]),
        pltpu.make_async_copy(inf, inf_held, sems.at[2]),
    ]
    for move in moves:
        move.start()
    moves[2].wait()
    lanes = inf_held[...]
    wide = jnp.concatenate([lanes] * (128 // lanes.shape[0]), axis=0).T
    spread[...] = wide
    gi[:, sens:] = wide.astype(BF16)
    moves[1].wait()
    moves[0].wait()


def extend(p_ref, t, q_ref):
    for n in range(0, t.shape[0], 256):
        q_ref[:, n : n + 256] = times(p_ref[...], t[:, n : n + 256]).astype(BF16)


def lag_group(shape):
    return (lax.broadcasted_iota(jnp.int32, shape, 1) & 31) >> 2


def weigh(p, gi, m, w, lag):
    sens = gi.shape[1] - 128
    value = times(p[...], gi[...])
    place = lag % 4 * sens
    m[:, place : place + sens] = value[:, :sens].astype(BF16)
    w[...] = jnp.where(lag_group(w.shape) == lag, value[:, sens:], w[...])


def first_kernel(near, c, gi, spread, q, m, w, t, p):
    sens = gi.shape[1] - 128
    j = position()
    build(c, record_of(j, 0, near), p)
    m[:, :sens] = gi[:, :sens]
    w[...] = spread[...]
    weigh(p, gi, m, w, 1)
    build(c, record_of(j, 1, near), t)
    extend(p, t, q)
    weigh(q, gi, m, w, 2)


def second_kernel(near, c, gi, p, m_in, w_in, q, m, w, t):
    sens = gi.shape[1] - 128
    build(c, record_of(position(), 2, near), t)
    m[:, : 3 * sens] = m_in[...]
    w[...] = w_in[...]
    extend(p, t, q)
    weigh(q, gi, m, w, 3)


def far_kernel(near, far, swapped, c, gi, f, fw, picks, t):
    sens = f.shape[1] // 3
    j = position()
    group = lag_group(fw.shape)
    f5, f6, f7 = (f.at[:, n * sens : (n + 1) * sens] for n in range(3))
    for lag in (6, 5, 4):
        build(c, record_of(j, lag, near, far, swapped), t)
        gain, spread = gi[:, :sens], gi[:, sens:]
        f7[...] = times(t[...], gain if lag == 6 else f7[...]).astype(BF16)
        if lag < 6:
            f6[...] = times(t[...], gain if lag == 5 else f6[...]).astype(BF16)
        if lag < 5:
            f5[...] = times(t[...], gain).astype(BF16)
        loads = spread if lag == 6 else jnp.where(group > lag + 1, fw[...], spread)
        fw[...] = times(t[...], loads).astype(BF16)
    fw[...] = jnp.where(group > 4, fw[...], gi[:, sens:])
    which = lax.broadcasted_iota(jnp.int32, (4, picks.shape[1]), 0).astype(F32)
    rows = [[], []]
    for lag in range(LAGS):
        rec = record_of(j, lag, near, far, swapped)
        mine = which == rec[5:6, :]
        for part in range(2):
            rows[part].append(jnp.where(mine, rec[6 + part : 7 + part, :], 0.0))
    high, low = (jnp.concatenate(r, axis=0).astype(BF16) for r in rows)
    for n, part in enumerate((high, low, high, jnp.zeros_like(low))):
        picks[32 * n : 32 * n + 32, :] = part


def near_kernel(near, c, gi, p, w_in, f, fw, m, t, q):
    sens = gi.shape[1] - 128
    build(c, record_of(position(), 3, near), t)
    extend(p, t, q)
    m[:, :sens] = times(q[...], gi[:, :sens]).astype(BF16)
    for n in range(3):
        right = f[:, n * sens : (n + 1) * sens]
        m[:, (n + 1) * sens : (n + 2) * sens] = times(q[...], right).astype(BF16)
    lanes = lax.broadcasted_iota(jnp.int32, w_in.shape, 1)
    full = jnp.where(lag_group(w_in.shape) > 3, times(q[...], fw[...]), w_in[...])
    high = full.astype(BF16)
    low = (full - high.astype(F32)).astype(BF16)
    m[:, 4 * sens :] = jnp.where(
        lanes < 64, high, jnp.where(lanes < 96, low, jnp.zeros_like(low))
    )


TABLE = {
    0: ["O", "CYR2", "YR1", "CR2", "R1", "Y6", "CZ3", "Z2"],
    1: ["O", "CO", "YR2", "CYR1", "R2", "CR1", "CY6", "Z3"],
    2: ["O", "CYO2", "YO1", "CR2", "R1", "CYR2", "YR1", "Z2"],
    3: ["O", "CO", "YO2", "CYO1", "R2", "CR1", "YR2", "CYR1"],
}


def sum_kernel(names, cols, *refs):
    blocks = dict(zip(names, refs[: len(names)]))
    close, distant, picks, out, outgoing, sems = refs[len(names) :]
    steps = out.shape[-1] // cols
    j = position()

    def columns(i):
        return pl.ds(pl.multiple_of(i * cols, cols), cols)

    def result(i, slot):
        return pltpu.make_async_copy(
            outgoing.at[slot], out.at[0, :, columns(i)], sems.at[slot]
        )

    for pos, held in TABLE.items():

        @pl.when(j == pos)
        def _(held=held):
            @pl.loop(0, steps)
            def _(i):
                now = lax.rem(i, 2)
                readings = [blocks[name][:, columns(i)] for name in held]
                total = times(close[...], jnp.concatenate(readings[:4], axis=0))
                rest = jnp.concatenate(readings[4:] + [picks[:, columns(i)]], axis=0)
                total += times(distant[...], rest)

                @pl.when(i >= 2)
                def _():
                    result(i - 2, now).wait()

                outgoing[now] = total
                result(i, now).start()

            for i in range(max(steps - 2, 0), steps):
                result(i, i % 2).wait()


def call_sum(blocks, close, distant, picks):
    names = sorted({name for held in TABLE.values() for name in held})
    width, scen = close.shape[0], picks.shape[1]
    cols = COLS
    return pl.pallas_call(
        functools.partial(sum_kernel, names, cols),
        out_shape=jax.ShapeDtypeStruct((1, width, scen), F32),
        in_specs=[VMEM] * (len(names) + 3),
        out_specs=ANY,
        scratch_shapes=[pltpu.VMEM((2, width, cols), F32), pltpu.SemaphoreType.DMA((2,))],
        cost_estimate=pl.CostEstimate(
            flops=2 * width * scen * (close.shape[1] + distant.shape[1]),
            bytes_accessed=16 * MIB,
            transcendentals=0,
        ),
        compiler_params=pltpu.CompilerParams(vmem_limit_bytes=LIMIT),
    )(*[blocks[n] for n in names], close, distant, picks)


def per_device(coupling, decay, block_mask, gain, readings, influence, lanes, axle_load):
    width, sens = gain.shape
    scen = readings.shape[2]
    core = lax.rem(lax.axis_index("tm"), 2)
    own = readings[0]
    shape = jax.ShapeDtypeStruct
    loads = shape((width, 128), F32)
    square = shape((width, width), BF16)
    unit = 2 * width * width * 256
    t_scratch = pltpu.VMEM((width, width), BF16)

    small = [decay, block_mask, lanes, axle_load]
    (record,) = call(
        record_kernel, [shape((1, ROWS, scen), BF16)], small,
        [pltpu.VMEM(a.shape, a.dtype) for a in small] + [pltpu.SemaphoreType.DMA((4,))],
        flops=MIB, spec=ANY, limit=56 * MIB,
    )
    r = {"O": own}
    r["R1"] = send(own, [(0, 0, 1), (2, 2, 1)])
    r["YO1"] = send(own, ROW0)
    r["CO"] = send(own, CORE)
    pair = jnp.concatenate([record, send(record, CORE)], axis=0)
    pairs = jnp.stack([pair, send(pair, [(1, 1, 1), (3, 3, 1)])])
    c, gi, spread = call(
        load_kernel, [square, shape((width, sens + 128), BF16), loads],
        [coupling, gain, influence.T],
        [pltpu.VMEM(influence.T.shape, F32), pltpu.SemaphoreType.DMA((3,))],
        flops=MIB, spec=ANY,
    )
    near = jnp.concatenate([pairs, send(pairs, ROW1)], axis=1)
    near = jnp.where(core == 1, near, send(near, CORE))
    near, r["R1"], r["YO1"], c = lax.optimization_barrier((near, r["R1"], r["YO1"], c))
    r["R2"] = send(after(own, pairs), [(1, 1, 1), (3, 3, 1)])
    far = send(near[1], [(0, 0, 1), (2, 2, 1)])
    far = (far, send(far, CORE))
    r1 = r["R1"]
    r["YR1"] = send(r1, ROW0)
    p2, close, w = call(
        first_kernel, [square, shape((width, 3 * sens), BF16), loads],
        [near, c, gi, spread], [t_scratch, t_scratch], flops=8 * unit,
    )
    p2, r2 = lax.optimization_barrier((p2, r["R2"]))
    r["R2"] = r2
    r["YR2"] = send(r2, ROW1)
    r["Z2"] = send(r2, [(1, 0, 1), (3, 2, 1)])
    r["CR2"] = send(r2, CORE)
    r["CR1"] = send(after(r1, p2), CORE)
    r["CYO1"] = send(after(r["YO1"], p2), CORE)
    p3, close, w = call(
        second_kernel, [square, shape((width, 4 * sens), BF16), loads],
        [near, c, gi, p2, close, w], [t_scratch], flops=6 * unit,
    )
    yr1 = r["YR1"] = after(r["YR1"], p3)
    r["Z3"] = send(yr1, [(0, 1, 1)])
    r["CYR1"] = send(yr1, CORE)
    far, r["CO"], r["CYO1"], r["CR1"], r["Z2"] = lax.optimization_barrier(
        (far, r["CO"], r["CYO1"], r["CR1"], r["Z2"], p3)
    )[:5]
    r["Y6"] = send(r["Z2"], [(2, 0, 0)])
    r["YO2"] = send(after(own, r["Z2"]), [(1, 3, 0)])
    f, fw, picks = call(
        far_kernel,
        [shape((width, 3 * sens), BF16), shape((width, 128), BF16), shape((128, scen), BF16)],
        [near, *far, c, gi], [t_scratch], flops=9 * unit,
    )
    p3, r["CYR1"], r["CR2"] = lax.optimization_barrier((p3, r["CYR1"], r["CR2"], f))[:3]
    r["CYR2"] = send(r["YR2"], CORE)
    (distant,) = call(
        near_kernel, [shape((width, 4 * sens + 128), BF16)],
        [near, c, gi, p3, w, f, fw], [t_scratch, t_scratch], flops=unit,
    )
    r["CZ3"] = send(after(r["Z3"], distant), CORE)
    r["CYO2"] = send(after(r["YO2"], distant), CORE)
    r["CY6"] = send(after(r["Y6"], distant), CORE)
    return call_sum(r, close, distant, picks)


def solution(mesh):
    placed = (
        P(),
        P(("groups", "tm"), None),
        P(("groups", "tm"), None, None),
        P(),
        P(("groups", "tm"), None, None),
        P(),
        P(("groups", "tm"), None),
        P(("groups", "tm"), None),
    )
    return jax.shard_map(
        per_device,
        mesh=mesh,
        in_specs=placed,
        out_specs=P(("groups", "tm"), None, None),
        check_vma=False,
    )
```

```python
import functools

import jax
import jax.numpy as jnp
from jax import lax
from jax.experimental import pallas as pl
from jax.experimental.pallas import tpu as pltpu
from jax.sharding import PartitionSpec as P

MIB = 1 << 20
LIMIT = 20 * MIB
VMEM = pl.BlockSpec(memory_space=pltpu.VMEM)
ANY = pl.BlockSpec(memory_space=pl.ANY)
F32 = jnp.float32
BF16 = jnp.bfloat16
LAGS = 8
COLS = 256
ROWS = 8


def position():
    return lax.rem(lax.axis_index("tm"), 4)


def send(block, pairs):
    count = lax.axis_size("tm")
    route = []
    for level in range(count // 4):
        for a, b, step in pairs:
            if level + step < count // 4:
                route.append((level * 4 + a, (level + step) * 4 + b))
    return lax.ppermute(block, "tm", route)


def after(block, *others):
    return lax.optimization_barrier((block, *others))[0]


CORE = [(0, 1, 0), (1, 0, 0), (2, 3, 0), (3, 2, 0)]
ROW = [(0, 2, 0), (2, 0, 0), (1, 3, 0), (3, 1, 0)]
ROW0 = [(0, 2, 0), (2, 0, 0)]
ALL = [(0, 0, 1), (1, 1, 1), (2, 2, 1), (3, 3, 1)]
ROW1 = [(1, 3, 0), (3, 1, 0)]


def record_of(j, lag, near, far=None, swapped=None):
    d = j - lag
    pos = lax.rem(d + 8, 4)
    row = jnp.where(d >= 0, near[0, pos ^ (j | 1)], near[1, pos ^ (j | 1)])
    if far is not None:
        held = jnp.where((j & 1) == 0, far[pos ^ (j | 1)], swapped[pos ^ (j | 1)])
        row = jnp.where(d >= -4, row, held)
    return row.astype(F32)


def call(kernel, outs, ins, scratch=(), flops=0, spec=VMEM, limit=LIMIT):
    moved = sum(a.size * a.dtype.itemsize for a in ins)
    return pl.pallas_call(
        kernel,
        out_shape=outs,
        in_specs=[spec] * len(ins),
        out_specs=[VMEM] * len(outs),
        scratch_shapes=list(scratch),
        cost_estimate=pl.CostEstimate(flops=flops, bytes_accessed=moved, transcendentals=0),
        compiler_params=pltpu.CompilerParams(vmem_limit_bytes=limit),
    )(*ins)


def build(c_ref, rec, t_ref):
    width = t_ref.shape[0]
    size = width // 8
    eye = (
        lax.broadcasted_iota(jnp.int32, (size, size), 0)
        == lax.broadcasted_iota(jnp.int32, (size, size), 1)
    ).astype(F32)
    for p in range(8):
        rows = slice(p * size, (p + 1) * size)
        half = p % 2 * width
        masked = c_ref[rows, :].astype(F32) * rec[p // 2 : p // 2 + 1, half : half + width]
        t_ref[rows, :] = masked.astype(BF16)
        rate = rec[4:5, p * size : (p + 1) * size]
        t_ref[rows, rows] = (masked[:, rows] + eye * rate).astype(BF16)


def times(left, right):
    return jnp.dot(left, right, preferred_element_type=F32)


def split(value, m, w):
    sens = m.shape[1]
    m[...] = value[:, :sens].astype(BF16)
    w[...] = value[:, sens:]


def record_kernel(decay, mask, lanes, load, out, *scratch):
    held, sems = scratch[:4], scratch[4]
    moves = [
        pltpu.make_async_copy(source, target, sems.at[i])
        for i, (source, target) in enumerate(zip((decay, mask, lanes, load), held))
    ]
    for move in moves:
        move.start()
    for move in moves:
        move.wait()
    decay, mask, lanes, load = held
    width = decay.shape[1]
    size = width // 8
    flags = mask[...]
    for q in range(8):
        wide = jnp.broadcast_to(flags[0, :, q : q + 1].astype(F32), (8, size)).astype(BF16)
        for p in range(8):
            first = p % 2 * width + q * size
            out[0, p // 2 : p // 2 + 1, first : first + size] = wide[p : p + 1]
    rate = decay[...]
    loads = load[...]
    high = loads.astype(BF16).astype(F32)
    rows = [jnp.concatenate([rate, jnp.zeros_like(rate)], axis=1)]
    rows += [lanes[...].astype(F32), high, loads - high]
    out[0, 4:, :] = jnp.concatenate(rows, axis=0).astype(BF16)


def load_kernel(c, gain, inf, c_out, gi, spread, inf_held, sems):
    sens = gain.shape[1]
    moves = [
        pltpu.make_async_copy(c, c_out, sems.at[0]),
        pltpu.make_async_copy(gain, gi.at[:, :sens], sems.at[1]),
        pltpu.make_async_copy(inf, inf_held, sems.at[2]),
    ]
    for move in moves:
        move.start()
    moves[2].wait()
    lanes = inf_held[...]
    wide = jnp.concatenate([lanes] * (128 // lanes.shape[0]), axis=0).T
    spread[...] = wide
    gi[:, sens:] = wide.astype(BF16)
    moves[1].wait()
    moves[0].wait()


def extend(p_ref, t, q_ref):
    for n in range(0, t.shape[0], 256):
        q_ref[:, n : n + 256] = times(p_ref[...], t[:, n : n + 256]).astype(BF16)


def lag_group(shape):
    return (lax.broadcasted_iota(jnp.int32, shape, 1) & 31) >> 2


def weigh(p, gi, m, w, lag):
    sens = gi.shape[1] - 128
    value = times(p[...], gi[...])
    place = lag % 4 * sens
    m[:, place : place + sens] = value[:, :sens].astype(BF16)
    w[...] = jnp.where(lag_group(w.shape) == lag, value[:, sens:], w[...])


def first_kernel(near, c, gi, spread, q, m, w, t, p):
    sens = gi.shape[1] - 128
    j = position()
    build(c, record_of(j, 0, near), p)
    m[:, :sens] = gi[:, :sens]
    w[...] = spread[...]
    weigh(p, gi, m, w, 1)
    build(c, record_of(j, 1, near), t)
    extend(p, t, q)
    weigh(q, gi, m, w, 2)


def second_kernel(near, c, gi, p, m_in, w_in, q, m, w, t):
    sens = gi.shape[1] - 128
    build(c, record_of(position(), 2, near), t)
    m[:, : 3 * sens] = m_in[...]
    w[...] = w_in[...]
    extend(p, t, q)
    weigh(q, gi, m, w, 3)


def far_kernel(near, far, swapped, c, gi, f, fw, picks, t):
    sens = f.shape[1] // 3
    j = position()
    group = lag_group(fw.shape)
    f5, f6, f7 = (f.at[:, n * sens : (n + 1) * sens] for n in range(3))
    for lag in (6, 5, 4):
        build(c, record_of(j, lag, near, far, swapped), t)
        gain, spread = gi[:, :sens], gi[:, sens:]
        f7[...] = times(t[...], gain if lag == 6 else f7[...]).astype(BF16)
        if lag < 6:
            f6[...] = times(t[...], gain if lag == 5 else f6[...]).astype(BF16)
        if lag < 5:
            f5[...] = times(t[...], gain).astype(BF16)
        loads = spread if lag == 6 else jnp.where(group > lag + 1, fw[...], spread)
        fw[...] = times(t[...], loads).astype(BF16)
    fw[...] = jnp.where(group > 4, fw[...], gi[:, sens:])
    which = lax.broadcasted_iota(jnp.int32, (4, picks.shape[1]), 0).astype(F32)
    rows = [[], []]
    for lag in range(LAGS):
        rec = record_of(j, lag, near, far, swapped)
        mine = which == rec[5:6, :]
        for part in range(2):
            rows[part].append(jnp.where(mine, rec[6 + part : 7 + part, :], 0.0))
    high, low = (jnp.concatenate(r, axis=0).astype(BF16) for r in rows)
    for n, part in enumerate((high, low, high, jnp.zeros_like(low))):
        picks[32 * n : 32 * n + 32, :] = part


def near_kernel(near, c, gi, p, w_in, f, fw, m, t, q):
    sens = gi.shape[1] - 128
    build(c, record_of(position(), 3, near), t)
    extend(p, t, q)
    m[:, :sens] = times(q[...], gi[:, :sens]).astype(BF16)
    for n in range(3):
        right = f[:, n * sens : (n + 1) * sens]
        m[:, (n + 1) * sens : (n + 2) * sens] = times(q[...], right).astype(BF16)
    lanes = lax.broadcasted_iota(jnp.int32, w_in.shape, 1)
    full = jnp.where(lag_group(w_in.shape) > 3, times(q[...], fw[...]), w_in[...])
    high = full.astype(BF16)
    low = (full - high.astype(F32)).astype(BF16)
    m[:, 4 * sens :] = jnp.where(
        lanes < 64, high, jnp.where(lanes < 96, low, jnp.zeros_like(low))
    )


TABLE = {
    0: ["O", "CYR2", "YR1", "CR2", "R1", "Y6", "CZ3", "Z2"],
    1: ["O", "CO", "YR2", "CYR1", "R2", "CR1", "CY6", "Z3"],
    2: ["O", "CYO2", "YO1", "CR2", "R1", "CYR2", "YR1", "Z2"],
    3: ["O", "CO", "YO2", "CYO1", "R2", "CR1", "YR2", "CYR1"],
}


def near_sum(names, cols, *refs):
    blocks = dict(zip(names, refs[: len(names)]))
    close, out = refs[len(names) :]
    j = position()
    for pos, held in TABLE.items():

        @pl.when(j == pos)
        def _(held=held):
            @pl.loop(0, out.shape[1] // cols)
            def _(i):
                where = pl.ds(pl.multiple_of(i * cols, cols), cols)
                readings = [blocks[name][:, where] for name in held[:4]]
                out[:, where] = times(close[...], jnp.concatenate(readings, axis=0))


def far_sum(names, cols, *refs):
    blocks = dict(zip(names, refs[: len(names)]))
    distant, picks, start, out, outgoing, sems = refs[len(names) :]
    steps = out.shape[-1] // cols
    j = position()

    def columns(i):
        return pl.ds(pl.multiple_of(i * cols, cols), cols)

    def result(i, slot):
        return pltpu.make_async_copy(
            outgoing.at[slot], out.at[0, :, columns(i)], sems.at[slot]
        )

    for pos, held in TABLE.items():

        @pl.when(j == pos)
        def _(held=held):
            @pl.loop(0, steps)
            def _(i):
                now = lax.rem(i, 2)
                readings = [blocks[name][:, columns(i)] for name in held[4:]]
                rest = jnp.concatenate(readings + [picks[:, columns(i)]], axis=0)

                @pl.when(i >= 2)
                def _():
                    result(i - 2, now).wait()

                outgoing[now] = start[:, columns(i)] + times(distant[...], rest)
                result(i, now).start()

            for i in range(max(steps - 2, 0), steps):
                result(i, i % 2).wait()


def names_of(part):
    return sorted({name for held in TABLE.values() for name in held[part]})


def call_near(blocks, close, scen):
    names = names_of(slice(0, 4))
    return pl.pallas_call(
        functools.partial(near_sum, names, COLS),
        out_shape=jax.ShapeDtypeStruct((close.shape[0], scen), F32),
        in_specs=[VMEM] * (len(names) + 1),
        out_specs=VMEM,
        cost_estimate=pl.CostEstimate(
            flops=MIB, bytes_accessed=MIB, transcendentals=0
        ),
        compiler_params=pltpu.CompilerParams(vmem_limit_bytes=LIMIT),
    )(*[blocks[n] for n in names], close)


def call_far(blocks, distant, picks, start):
    names = names_of(slice(4, 8))
    width, scen = start.shape
    return pl.pallas_call(
        functools.partial(far_sum, names, COLS),
        out_shape=jax.ShapeDtypeStruct((1, width, scen), F32),
        in_specs=[VMEM] * (len(names) + 3),
        out_specs=ANY,
        scratch_shapes=[pltpu.VMEM((2, width, COLS), F32), pltpu.SemaphoreType.DMA((2,))],
        cost_estimate=pl.CostEstimate(
            flops=2 * scen * distant.size, bytes_accessed=16 * MIB, transcendentals=0
        ),
        compiler_params=pltpu.CompilerParams(vmem_limit_bytes=LIMIT),
    )(*[blocks[n] for n in names], distant, picks, start)


def per_device(coupling, decay, block_mask, gain, readings, influence, lanes, axle_load):
    width, sens = gain.shape
    scen = readings.shape[2]
    core = lax.rem(lax.axis_index("tm"), 2)
    own = readings[0]
    shape = jax.ShapeDtypeStruct
    loads = shape((width, 128), F32)
    square = shape((width, width), BF16)
    unit = 2 * width * width * 256
    t_scratch = pltpu.VMEM((width, width), BF16)

    small = [decay, block_mask, lanes, axle_load]
    (record,) = call(
        record_kernel, [shape((1, ROWS, scen), BF16)], small,
        [pltpu.VMEM(a.shape, a.dtype) for a in small] + [pltpu.SemaphoreType.DMA((4,))],
        flops=MIB, spec=ANY, limit=56 * MIB,
    )
    r = {"O": own}
    r["R1"] = send(own, [(0, 0, 1), (2, 2, 1)])
    r["YO1"] = send(own, ROW0)
    r["CO"] = send(own, CORE)
    pair = jnp.concatenate([record, send(record, CORE)], axis=0)
    pairs = jnp.stack([pair, send(pair, [(1, 1, 1), (3, 3, 1)])])
    near = jnp.concatenate([pairs, send(pairs, ROW1)], axis=1)
    near = jnp.where(core == 1, near, send(near, CORE))
    late = lax.optimization_barrier((near, coupling, gain, influence.T))
    near = late[0]
    c, gi, spread = call(
        load_kernel, [square, shape((width, sens + 128), BF16), loads],
        list(late[1:]),
        [pltpu.VMEM(influence.T.shape, F32), pltpu.SemaphoreType.DMA((3,))],
        flops=MIB, spec=ANY,
    )
    near, r["R1"], c = lax.optimization_barrier((near, r["R1"], c))
    r["R2"] = send(after(own, pairs), [(1, 1, 1), (3, 3, 1)])
    r1 = r["R1"]
    far = send(near[1], [(0, 0, 1), (2, 2, 1)])
    r["YR1"] = send(r1, ROW0)
    near, r["YO1"] = lax.optimization_barrier((near, r["YO1"]))
    p2, close, w = call(
        first_kernel, [square, shape((width, 3 * sens), BF16), loads],
        [near, c, gi, spread], [t_scratch, t_scratch], flops=8 * unit,
    )
    p2, r2 = lax.optimization_barrier((p2, r["R2"]))
    r["R2"] = r2
    r["YR2"] = send(r2, ROW1)
    r["Z2"] = send(r2, [(1, 0, 1), (3, 2, 1)])
    r["CR2"] = send(r2, CORE)
    r["CR1"] = send(after(r1, p2), CORE)
    r["CYO1"] = send(after(r["YO1"], p2), CORE)
    r["YO2"] = send(after(own, p2), [(1, 3, 0)])
    p2, r["YR1"], far = lax.optimization_barrier((p2, r["YR1"], far))
    p3, close, w = call(
        second_kernel, [square, shape((width, 4 * sens), BF16), loads],
        [near, c, gi, p2, close, w], [t_scratch], flops=6 * unit,
    )
    yr1 = r["YR1"] = after(r["YR1"], p3)
    far = (far, send(after(far, p3), CORE))
    r["Z3"] = send(yr1, [(0, 1, 1)])
    r["CYR1"] = send(yr1, CORE)
    far, r["CO"], r["CYO1"], r["CR1"], r["YR2"], r["Z2"] = lax.optimization_barrier(
        (far, r["CO"], r["CYO1"], r["CR1"], r["YR2"], r["Z2"], p3)
    )[:6]
    r["Y6"] = send(r["Z2"], [(2, 0, 0)])
    f, fw, picks = call(
        far_kernel,
        [shape((width, 3 * sens), BF16), shape((width, 128), BF16), shape((128, scen), BF16)],
        [near, *far, c, gi], [t_scratch], flops=4 * unit,
    )
    r["CYO2"] = send(after(r["YO2"], f), CORE)
    p3, r["CYR1"], r["CR2"] = lax.optimization_barrier((p3, r["CYR1"], r["CR2"], f))[:3]
    r["CYR2"] = send(r["YR2"], CORE)
    (distant,) = call(
        near_kernel, [shape((width, 4 * sens + 128), BF16)],
        [near, c, gi, p3, w, f, fw], [t_scratch, t_scratch], flops=MIB,
    )
    r["CZ3"] = send(after(r["Z3"], distant), CORE)
    close, r["Y6"] = lax.optimization_barrier((close, r["Y6"], distant))[:2]
    r["CY6"] = send(r["Y6"], CORE)
    start = call_near(r, close, scen)
    return call_far(r, distant, picks, start)


def solution(mesh):
    placed = (
        P(),
        P(("groups", "tm"), None),
        P(("groups", "tm"), None, None),
        P(),
        P(("groups", "tm"), None, None),
        P(),
        P(("groups", "tm"), None),
        P(("groups", "tm"), None),
    )
    return jax.shard_map(
        per_device,
        mesh=mesh,
        in_specs=placed,
        out_specs=P(("groups", "tm"), None, None),
        check_vma=False,
    )
```

```python
import functools

import jax
import jax.numpy as jnp
from jax import lax
from jax.experimental import pallas as pl
from jax.experimental.pallas import tpu as pltpu
from jax.sharding import PartitionSpec as P

MIB = 1 << 20
LIMIT = 20 * MIB
VMEM = pl.BlockSpec(memory_space=pltpu.VMEM)
ANY = pl.BlockSpec(memory_space=pl.ANY)
F32 = jnp.float32
BF16 = jnp.bfloat16
LAGS = 8
COLS = 512
ROWS = 8


def position():
    return lax.rem(lax.axis_index("tm"), 4)


def send(block, pairs):
    count = lax.axis_size("tm")
    route = []
    for level in range(count // 4):
        for a, b, step in pairs:
            if level + step < count // 4:
                route.append((level * 4 + a, (level + step) * 4 + b))
    return lax.ppermute(block, "tm", route)


def after(block, *others):
    return lax.optimization_barrier((block, *others))[0]


CORE = [(0, 1, 0), (1, 0, 0), (2, 3, 0), (3, 2, 0)]
ROW = [(0, 2, 0), (2, 0, 0), (1, 3, 0), (3, 1, 0)]
ROW0 = [(0, 2, 0), (2, 0, 0)]
ALL = [(0, 0, 1), (1, 1, 1), (2, 2, 1), (3, 3, 1)]
ROW1 = [(1, 3, 0), (3, 1, 0)]


def record_of(j, lag, near, far=None, swapped=None):
    d = j - lag
    pos = lax.rem(d + 8, 4)
    row = jnp.where(d >= 0, near[0, pos ^ (j | 1)], near[1, pos ^ (j | 1)])
    if far is not None:
        held = jnp.where((j & 1) == 0, far[pos ^ (j | 1)], swapped[pos ^ (j | 1)])
        row = jnp.where(d >= -4, row, held)
    return row.astype(F32)


def call(kernel, outs, ins, scratch=(), flops=0, spec=VMEM, limit=LIMIT):
    moved = sum(a.size * a.dtype.itemsize for a in ins)
    return pl.pallas_call(
        kernel,
        out_shape=outs,
        in_specs=[spec] * len(ins),
        out_specs=[VMEM] * len(outs),
        scratch_shapes=list(scratch),
        cost_estimate=pl.CostEstimate(flops=flops, bytes_accessed=moved, transcendentals=0),
        compiler_params=pltpu.CompilerParams(vmem_limit_bytes=limit),
    )(*ins)


def build(c_ref, rec, t_ref):
    width = t_ref.shape[0]
    size = width // 8
    eye = (
        lax.broadcasted_iota(jnp.int32, (size, size), 0)
        == lax.broadcasted_iota(jnp.int32, (size, size), 1)
    ).astype(F32)
    for p in range(8):
        rows = slice(p * size, (p + 1) * size)
        half = p % 2 * width
        masked = c_ref[rows, :].astype(F32) * rec[p // 2 : p // 2 + 1, half : half + width]
        t_ref[rows, :] = masked.astype(BF16)
        rate = rec[4:5, p * size : (p + 1) * size]
        t_ref[rows, rows] = (masked[:, rows] + eye * rate).astype(BF16)


def times(left, right):
    return jnp.dot(left, right, preferred_element_type=F32)


def split(value, m, w):
    sens = m.shape[1]
    m[...] = value[:, :sens].astype(BF16)
    w[...] = value[:, sens:]


def record_kernel(decay, mask, lanes, load, out, *scratch):
    held, sems = scratch[:4], scratch[4]
    moves = [
        pltpu.make_async_copy(source, target, sems.at[i])
        for i, (source, target) in enumerate(zip((decay, mask, lanes, load), held))
    ]
    for move in moves:
        move.start()
    for move in moves:
        move.wait()
    decay, mask, lanes, load = held
    width = decay.shape[1]
    size = width // 8
    flags = mask[...]
    for q in range(8):
        wide = jnp.broadcast_to(flags[0, :, q : q + 1].astype(F32), (8, size)).astype(BF16)
        for p in range(8):
            first = p % 2 * width + q * size
            out[0, p // 2 : p // 2 + 1, first : first + size] = wide[p : p + 1]
    rate = decay[...]
    loads = load[...]
    high = loads.astype(BF16).astype(F32)
    rows = [jnp.concatenate([rate, jnp.zeros_like(rate)], axis=1)]
    rows += [lanes[...].astype(F32), high, loads - high]
    out[0, 4:, :] = jnp.concatenate(rows, axis=0).astype(BF16)


def load_kernel(c, gain, inf, c_out, gi, spread, inf_held, sems):
    sens = gain.shape[1]
    moves = [
        pltpu.make_async_copy(c, c_out, sems.at[0]),
        pltpu.make_async_copy(gain, gi.at[:, :sens], sems.at[1]),
        pltpu.make_async_copy(inf, inf_held, sems.at[2]),
    ]
    for move in moves:
        move.start()
    moves[2].wait()
    lanes = inf_held[...]
    wide = jnp.concatenate([lanes] * (128 // lanes.shape[0]), axis=0).T
    spread[...] = wide
    gi[:, sens:] = wide.astype(BF16)
    moves[1].wait()
    moves[0].wait()


def extend(p_ref, t, q_ref):
    for n in range(0, t.shape[0], 256):
        q_ref[:, n : n + 256] = times(p_ref[...], t[:, n : n + 256]).astype(BF16)


def lag_group(shape):
    return (lax.broadcasted_iota(jnp.int32, shape, 1) & 31) >> 2


def weigh(p, gi, m, w, lag):
    sens = gi.shape[1] - 128
    value = times(p[...], gi[...])
    place = lag % 4 * sens
    m[:, place : place + sens] = value[:, :sens].astype(BF16)
    w[...] = jnp.where(lag_group(w.shape) == lag, value[:, sens:], w[...])


def first_kernel(near, c, gi, spread, q, m, w, t, p):
    sens = gi.shape[1] - 128
    j = position()
    build(c, record_of(j, 0, near), p)
    m[:, :sens] = gi[:, :sens]
    w[...] = spread[...]
    weigh(p, gi, m, w, 1)
    build(c, record_of(j, 1, near), t)
    extend(p, t, q)
    weigh(q, gi, m, w, 2)


def second_kernel(near, c, gi, p, m_in, w_in, q, m, w, t):
    sens = gi.shape[1] - 128
    build(c, record_of(position(), 2, near), t)
    m[:, : 3 * sens] = m_in[...]
    w[...] = w_in[...]
    extend(p, t, q)
    weigh(q, gi, m, w, 3)


def far_kernel(near, far, swapped, c, gi, f, fw, picks, t):
    sens = f.shape[1] // 3
    j = position()
    group = lag_group(fw.shape)
    f5, f6, f7 = (f.at[:, n * sens : (n + 1) * sens] for n in range(3))
    for lag in (6, 5, 4):
        build(c, record_of(j, lag, near, far, swapped), t)
        gain, spread = gi[:, :sens], gi[:, sens:]
        f7[...] = times(t[...], gain if lag == 6 else f7[...]).astype(BF16)
        if lag < 6:
            f6[...] = times(t[...], gain if lag == 5 else f6[...]).astype(BF16)
        if lag < 5:
            f5[...] = times(t[...], gain).astype(BF16)
        loads = spread if lag == 6 else jnp.where(group > lag + 1, fw[...], spread)
        fw[...] = times(t[...], loads).astype(BF16)
    fw[...] = jnp.where(group > 4, fw[...], gi[:, sens:])
    which = lax.broadcasted_iota(jnp.int32, (4, picks.shape[1]), 0).astype(F32)
    rows = [[], []]
    for lag in range(LAGS):
        rec = record_of(j, lag, near, far, swapped)
        mine = which == rec[5:6, :]
        for part in range(2):
            rows[part].append(jnp.where(mine, rec[6 + part : 7 + part, :], 0.0))
    high, low = (jnp.concatenate(r, axis=0).astype(BF16) for r in rows)
    for n, part in enumerate((high, low, high, jnp.zeros_like(low))):
        picks[32 * n : 32 * n + 32, :] = part


def near_kernel(near, c, gi, p, w_in, f, fw, m, t, q):
    sens = gi.shape[1] - 128
    build(c, record_of(position(), 3, near), t)
    extend(p, t, q)
    m[:, :sens] = times(q[...], gi[:, :sens]).astype(BF16)
    for n in range(3):
        right = f[:, n * sens : (n + 1) * sens]
        m[:, (n + 1) * sens : (n + 2) * sens] = times(q[...], right).astype(BF16)
    lanes = lax.broadcasted_iota(jnp.int32, w_in.shape, 1)
    full = jnp.where(lag_group(w_in.shape) > 3, times(q[...], fw[...]), w_in[...])
    high = full.astype(BF16)
    low = (full - high.astype(F32)).astype(BF16)
    m[:, 4 * sens :] = jnp.where(
        lanes < 64, high, jnp.where(lanes < 96, low, jnp.zeros_like(low))
    )


TABLE = {
    0: ["O", "CYR2", "YR1", "CR2", "R1", "Y6", "CZ3", "Z2"],
    1: ["O", "CO", "YR2", "CYR1", "R2", "CR1", "CY6", "Z3"],
    2: ["O", "CYO2", "YO1", "CR2", "R1", "CYR2", "YR1", "Z2"],
    3: ["O", "CO", "YO2", "CYO1", "R2", "CR1", "YR2", "CYR1"],
}


def near_sum(names, cols, *refs):
    blocks = dict(zip(names, refs[: len(names)]))
    close, out = refs[len(names) :]
    j = position()
    for pos, held in TABLE.items():

        @pl.when(j == pos)
        def _(held=held):
            @pl.loop(0, out.shape[1] // cols)
            def _(i):
                where = pl.ds(pl.multiple_of(i * cols, cols), cols)
                readings = [blocks[name][:, where] for name in held[:4]]
                out[:, where] = times(close[...], jnp.concatenate(readings, axis=0))


def far_sum(names, cols, *refs):
    blocks = dict(zip(names, refs[: len(names)]))
    distant, picks, start, out, outgoing, sems = refs[len(names) :]
    steps = out.shape[-1] // cols
    j = position()

    def columns(i):
        return pl.ds(pl.multiple_of(i * cols, cols), cols)

    def result(i, slot):
        return pltpu.make_async_copy(
            outgoing.at[slot], out.at[0, :, columns(i)], sems.at[slot]
        )

    for pos, held in TABLE.items():

        @pl.when(j == pos)
        def _(held=held):
            @pl.loop(0, steps)
            def _(i):
                now = lax.rem(i, 2)
                readings = [blocks[name][:, columns(i)] for name in held[4:]]
                rest = jnp.concatenate(readings + [picks[:, columns(i)]], axis=0)

                @pl.when(i >= 2)
                def _():
                    result(i - 2, now).wait()

                outgoing[now] = start[:, columns(i)] + times(distant[...], rest)
                result(i, now).start()

            for i in range(max(steps - 2, 0), steps):
                result(i, i % 2).wait()


def names_of(part):
    return sorted({name for held in TABLE.values() for name in held[part]})


def call_near(blocks, close, scen):
    names = names_of(slice(0, 4))
    return pl.pallas_call(
        functools.partial(near_sum, names, COLS),
        out_shape=jax.ShapeDtypeStruct((close.shape[0], scen), F32),
        in_specs=[VMEM] * (len(names) + 1),
        out_specs=VMEM,
        cost_estimate=pl.CostEstimate(
            flops=MIB, bytes_accessed=MIB, transcendentals=0
        ),
        compiler_params=pltpu.CompilerParams(vmem_limit_bytes=LIMIT),
    )(*[blocks[n] for n in names], close)


def call_far(blocks, distant, picks, start):
    names = names_of(slice(4, 8))
    width, scen = start.shape
    return pl.pallas_call(
        functools.partial(far_sum, names, COLS),
        out_shape=jax.ShapeDtypeStruct((1, width, scen), F32),
        in_specs=[VMEM] * (len(names) + 3),
        out_specs=ANY,
        scratch_shapes=[pltpu.VMEM((2, width, COLS), F32), pltpu.SemaphoreType.DMA((2,))],
        cost_estimate=pl.CostEstimate(
            flops=2 * scen * distant.size, bytes_accessed=16 * MIB, transcendentals=0
        ),
        compiler_params=pltpu.CompilerParams(vmem_limit_bytes=LIMIT),
    )(*[blocks[n] for n in names], distant, picks, start)


def per_device(coupling, decay, block_mask, gain, readings, influence, lanes, axle_load):
    width, sens = gain.shape
    scen = readings.shape[2]
    core = lax.rem(lax.axis_index("tm"), 2)
    own = readings[0]
    shape = jax.ShapeDtypeStruct
    loads = shape((width, 128), F32)
    square = shape((width, width), BF16)
    unit = 2 * width * width * 256
    t_scratch = pltpu.VMEM((width, width), BF16)

    small = [decay, block_mask, lanes, axle_load]
    (record,) = call(
        record_kernel, [shape((1, ROWS, scen), BF16)], small,
        [pltpu.VMEM(a.shape, a.dtype) for a in small] + [pltpu.SemaphoreType.DMA((4,))],
        flops=MIB, spec=ANY, limit=56 * MIB,
    )
    r = {"O": own}
    r["R1"] = send(own, [(0, 0, 1), (2, 2, 1)])
    r["YO1"] = send(own, ROW0)
    r["CO"] = send(own, CORE)
    pair = jnp.concatenate([record, send(record, CORE)], axis=0)
    pairs = jnp.stack([pair, send(pair, [(1, 1, 1), (3, 3, 1)])])
    near = jnp.concatenate([pairs, send(pairs, ROW1)], axis=1)
    near = jnp.where(core == 1, near, send(near, CORE))
    late = lax.optimization_barrier((near, coupling, gain, influence.T))
    near = late[0]
    c, gi, spread = call(
        load_kernel, [square, shape((width, sens + 128), BF16), loads],
        list(late[1:]),
        [pltpu.VMEM(influence.T.shape, F32), pltpu.SemaphoreType.DMA((3,))],
        flops=MIB, spec=ANY,
    )
    near, r["R1"], c = lax.optimization_barrier((near, r["R1"], c))
    r["R2"] = send(after(own, pairs), [(1, 1, 1), (3, 3, 1)])
    r1 = r["R1"]
    far = send(near[1], [(0, 0, 1), (2, 2, 1)])
    r["YR1"] = send(r1, ROW0)
    near, r["YO1"] = lax.optimization_barrier((near, r["YO1"]))
    p2, close, w = call(
        first_kernel, [square, shape((width, 3 * sens), BF16), loads],
        [near, c, gi, spread], [t_scratch, t_scratch], flops=8 * unit,
    )
    p2, r2 = lax.optimization_barrier((p2, r["R2"]))
    r["R2"] = r2
    r["YR2"] = send(r2, ROW1)
    r["Z2"] = send(r2, [(1, 0, 1), (3, 2, 1)])
    r["CR2"] = send(r2, CORE)
    r["CR1"] = send(after(r1, p2), CORE)
    r["CYO1"] = send(after(r["YO1"], p2), CORE)
    r["YO2"] = send(after(own, p2), [(1, 3, 0)])
    p2, r["YR1"], far = lax.optimization_barrier((p2, r["YR1"], far))
    p3, close, w = call(
        second_kernel, [square, shape((width, 4 * sens), BF16), loads],
        [near, c, gi, p2, close, w], [t_scratch], flops=6 * unit,
    )
    yr1 = r["YR1"] = after(r["YR1"], p3)
    far = (far, send(after(far, p3), CORE))
    r["Z3"] = send(yr1, [(0, 1, 1)])
    r["CYR1"] = send(yr1, CORE)
    far, r["CO"], r["CYO1"], r["CR1"], r["YR2"], r["Z2"] = lax.optimization_barrier(
        (far, r["CO"], r["CYO1"], r["CR1"], r["YR2"], r["Z2"], p3)
    )[:6]
    r["Y6"] = send(r["Z2"], [(2, 0, 0)])
    f, fw, picks = call(
        far_kernel,
        [shape((width, 3 * sens), BF16), shape((width, 128), BF16), shape((128, scen), BF16)],
        [near, *far, c, gi], [t_scratch], flops=4 * unit,
    )
    r["CYO2"] = send(after(r["YO2"], f), CORE)
    p3, r["CYR1"], r["CR2"] = lax.optimization_barrier((p3, r["CYR1"], r["CR2"], f))[:3]
    r["CYR2"] = send(r["YR2"], CORE)
    (distant,) = call(
        near_kernel, [shape((width, 4 * sens + 128), BF16)],
        [near, c, gi, p3, w, f, fw], [t_scratch, t_scratch], flops=MIB,
    )
    r["CZ3"] = send(after(r["Z3"], distant), CORE)
    close, r["Y6"] = lax.optimization_barrier((close, r["Y6"], distant))[:2]
    r["CY6"] = send(r["Y6"], CORE)
    start = call_near(r, close, scen)
    return call_far(r, distant, picks, start)


def solution(mesh):
    placed = (
        P(),
        P(("groups", "tm"), None),
        P(("groups", "tm"), None, None),
        P(),
        P(("groups", "tm"), None, None),
        P(),
        P(("groups", "tm"), None),
        P(("groups", "tm"), None),
    )
    return jax.shard_map(
        per_device,
        mesh=mesh,
        in_specs=placed,
        out_specs=P(("groups", "tm"), None, None),
        check_vma=False,
    )
```
